32 devices in a mesh: depth: 2 (over core), tile: 16 (over z, y, x).
Axes of the slice: x: 2, y: 2, z: 4, core: 2. Of those that a mesh axis runs over, the one named last changes fastest.
Arguments:
- specimen: float32 [4, 2, 2048, 2048], P('depth', None, 'tile'), may hold values from -4.2 to 4.2
- scan_offsets: int32 [32, 2], P('tile'), may hold values from 0 to 1792, as said below
- probe_wave: float32 [2, 256, 256], replicated, may hold values from -4.2 to 4.2
- fresnel_phase: float32 [256, 256], replicated, may hold values from -3.140625 to 3.140625
- measured: float32 [32, 256, 256], P('tile'), may hold values from 0 to 3
Outputs:
- specimen_gradient: float32 [4, 2, 2048, 2048], P('depth', None, 'tile')
The draws below stay inside these ranges and needn't reach their ends.
Inputs may be any that keep to these rules, and one draw needn't show every extreme that they name: `scan_offsets`: A position held by tile index d (positions d * 2 to (d + 1) * 2 - 1) has its top row between max(0, (d - 1) * 128) and min(d * 128, 1792), and its left column at most 1792.
All inputs are finite; a program needn't handle non-finite values.
Results may differ from the reference program's by a relative error of at most 0.0003.
Values sent between devices are 32-bit elements; how exact they have to be, the bound alone decides.
No kernel may reach another device: no remote copies, remote signals or barrier semaphores. Data moves between devices by JAX's collectives and lax.ppermute only.
A program may use at most 128 MiB of HBM per device.

```python
import jax
import jax.numpy as jnp
from jax import lax

PSZ = 256
P_DEV = 2
OBJ_W = 2048
ROWS_DEV = 128
NROWS = 2048
SLICES = 4
POSITIONS = 32


def draw_scan_offsets(key, part):
    row_key = jax.random.fold_in(key, 11)
    col_key = jax.random.fold_in(key, 23)
    holder = jnp.arange(POSITIONS, dtype=jnp.int32) // P_DEV
    lowest = jnp.maximum(0, (holder - 1) * ROWS_DEV)
    highest = jnp.minimum(holder * ROWS_DEV, NROWS - PSZ)
    top_rows = jax.random.randint(row_key, (POSITIONS,), lowest, highest + 1)
    left_cols = jax.random.randint(col_key, (POSITIONS,), 0, OBJ_W - PSZ + 1)
    return jnp.stack([top_rows, left_cols], 1).astype(jnp.int32)


def block_scale(own_key, dims, split, smallest, top_value):
    gain = 1.0
    for dim, shards_of in split:
        heights = jax.random.uniform(jax.random.fold_in(jax.random.fold_in(own_key, 6), dim), (shards_of,), jnp.float32, smallest / len(split), top_value / len(split))
        gain = gain * jnp.repeat(jnp.exp(heights), dims[dim] // shards_of).reshape((-1,) + (1,) * (len(dims) - 1 - dim))
    return gain


def bell_draw(key, dims, scale, reach, shards=(), kind=jnp.bfloat16):
    level = block_scale(key, dims, shards, -0.22, 0.18) if shards else 1.0
    array = jax.random.normal(key, dims, jnp.float32) * scale * level
    return jnp.minimum(jnp.maximum(array, -reach), reach).astype(kind)


def setup_inputs(seed: int = 0) -> dict:
    key_of = jax.random.split(jax.random.key(seed), 6)
    specimen = bell_draw(key_of[0], (SLICES, 2, NROWS, OBJ_W), 0.7, 4.2, ((0, 2), (2, 16)), jnp.float32)
    scan_offsets = draw_scan_offsets(jax.random.fold_in(key_of[5], 71), 0)
    probe_wave = bell_draw(key_of[2], (2, PSZ, PSZ), 0.7, 4.2, (), jnp.float32)
    fresnel_phase = jnp.clip(jax.random.uniform(key_of[3], (PSZ, PSZ), jnp.float32, -3.140625, 3.140625), -3.140625, 3.140625)
    measured = jnp.clip(3.0 * jax.random.uniform(key_of[4], (POSITIONS, PSZ, PSZ), jnp.float32) ** block_scale(key_of[4], (POSITIONS, PSZ, PSZ), ((0, 16),), -0.2, 0.2), 0.0, 3.0)
    return dict(specimen=specimen, scan_offsets=scan_offsets, probe_wave=probe_wave, fresnel_phase=fresnel_phase, measured=measured)


def reference(specimen, scan_offsets, probe_wave, fresnel_phase, measured):
    layers = specimen.shape[0]
    complex_field = lax.complex(specimen[:, 0], specimen[:, 1])
    probe_complex = lax.complex(probe_wave[0], probe_wave[1])
    kernel = lax.complex(jnp.cos(fresnel_phase), jnp.sin(fresnel_phase))

    def forward(values):
        return jnp.fft.fft2(values, norm="ortho")

    def inverse(values):
        return jnp.fft.ifft2(values, norm="ortho")

    def one_position(gradient, inputs):
        offsets, target = inputs
        anchor = jnp.zeros((), jnp.int32)
        start = (anchor, offsets[0].astype(jnp.int32), offsets[1].astype(jnp.int32))
        patches = lax.dynamic_slice(complex_field, start, (layers, PSZ, PSZ))
        current = probe_complex
        wave_list = []
        passed = current
        for layer_index in range(layers):
            wave_list.append(current)
            passed = current * patches[layer_index]
            if layer_index + 1 < layers:
                current = inverse(kernel * forward(passed))
        spectrum = forward(passed)
        residue = 2.0 * (jnp.real(spectrum) ** 2 + jnp.imag(spectrum) ** 2 - target)
        current = inverse(residue * spectrum)
        grad_list = [None] * layers
        for layer_index in reversed(range(layers)):
            grad_list[layer_index] = jnp.conj(wave_list[layer_index]) * current
            if layer_index > 0:
                current = inverse(jnp.conj(kernel) * forward(jnp.conj(patches[layer_index]) * current))
        update = jnp.stack(grad_list, 0)
        region = lax.dynamic_slice(gradient, start, (layers, PSZ, PSZ))
        gradient = lax.dynamic_update_slice(gradient, region + update, start)
        return gradient, None

    gradient, unused = lax.scan(one_position, jnp.zeros_like(complex_field), (scan_offsets.astype(jnp.int32), measured))
    return jnp.stack([jnp.real(gradient), jnp.imag(gradient)], 1)
```

```python
import functools

import jax
import jax.numpy as jnp
import numpy as np
from jax import lax
from jax.experimental import pallas as pl
from jax.experimental.pallas import tpu as pltpu
from jax.sharding import PartitionSpec as P

F32 = jnp.float32
BF16 = jnp.bfloat16
AXES = ("depth", "tile")
ANY = pl.BlockSpec(memory_space=pl.ANY)
VMEM = pl.BlockSpec(memory_space=pltpu.VMEM)
SMEM = pl.BlockSpec(memory_space=pltpu.SMEM)
cat = jnp.concatenate


def dft_tables(extent):
    half = extent // 2
    row, col = np.arange(half)[:, None], np.arange(half)[None, :]
    blocks = []
    for parity in (0, 1):
        turn = (row * (2 * col + parity)) % extent
        wave = np.exp(-2j * np.pi * turn / extent) / np.sqrt(extent)
        blocks.append(np.block([[wave.real, wave.imag], [-wave.imag, wave.real]]))
    table = np.stack([blocks[0], blocks[1], blocks[0].T, blocks[1].T])
    high = table.astype(np.float32).astype(BF16)
    low = (table - high.astype(np.float64)).astype(np.float32).astype(BF16)
    return np.stack([high, low], 1)


def split(x):
    high = x.astype(BF16)
    return high, (x - high.astype(F32)).astype(BF16)


def dot(a, b):
    return jnp.dot(a, b, preferred_element_type=F32)


def rmul(x, table, which):
    high, low = split(x)
    t_high, t_low = table[which, 0], table[which, 1]
    return dot(high, t_high) + (dot(low, t_high) + dot(high, t_low))


def lmul(table, which, x):
    high, low = split(x)
    t_high, t_low = table[which, 0], table[which, 1]
    return dot(t_high, high) + (dot(t_high, low) + dot(t_low, high))


def forward(xr, xi, table):
    h = xr.shape[0] // 2
    e = rmul(cat([xr[:, :h] + xr[:, h:], xi[:, :h] + xi[:, h:]], 1), table, 0)
    o = rmul(cat([xr[:, :h] - xr[:, h:], xi[:, :h] - xi[:, h:]], 1), table, 1)
    yr, yi = cat([e[:, :h], o[:, :h]], 1), cat([e[:, h:], o[:, h:]], 1)
    e = lmul(table, 2, cat([yr[:h] + yr[h:], yi[:h] + yi[h:]], 0))
    o = lmul(table, 3, cat([yr[:h] - yr[h:], yi[:h] - yi[h:]], 0))
    return cat([e[:h], o[:h]], 0), cat([e[h:], o[h:]], 0)


def inverse(xr, xi, table):
    h = xr.shape[0] // 2
    e = lmul(table, 0, cat([xr[:h], xi[:h]], 0))
    o = lmul(table, 1, cat([xr[h:], xi[h:]], 0))
    yr = cat([e[:h] + o[:h], e[:h] - o[:h]], 0)
    yi = cat([e[h:] + o[h:], e[h:] - o[h:]], 0)
    e = rmul(cat([yr[:, :h], yi[:, :h]], 1), table, 2)
    o = rmul(cat([yr[:, h:], yi[:, h:]], 1), table, 3)
    return (
        cat([e[:, :h] + o[:, :h], e[:, :h] - o[:, :h]], 1),
        cat([e[:, h:] + o[:, h:], e[:, h:] - o[:, h:]], 1),
    )


def times(ref, a, b, conj):
    pr, pi = ref[0], ref[1]
    if conj:
        return pr * a + pi * b, pr * b - pi * a
    return pr * a - pi * b, pr * b + pi * a


def extract_kernel(count, cols_ref, *refs):
    blocks, outs = refs[: 2 * count], refs[2 * count :]
    lane = lax.broadcasted_iota(jnp.int32, outs[0].shape[2:], 1)
    for i in range(count):
        shift = cols_ref[i] % outs[0].shape[3]
        outs[i][0, 0] = jnp.where(lane < shift, blocks[2 * i + 1][0, 0], blocks[2 * i][0, 0])


def extract(specimen, cols, patch):
    count = cols.shape[0]
    layers, parts, rows, width = specimen.shape
    last = width // patch - 1

    def spec(i, step):
        def index(s, c, cols_ref):
            return s, c, 0, jnp.minimum(cols_ref[i] // patch + step, last)

        return pl.BlockSpec((1, 1, rows, patch), index)

    out = pl.BlockSpec((1, 1, rows, patch), lambda s, c, cols_ref: (s, c, 0, 0))
    size = layers * parts * rows * patch * 4
    return pl.pallas_call(
        functools.partial(extract_kernel, count),
        out_shape=[jax.ShapeDtypeStruct((layers, parts, rows, patch), F32)] * count,
        grid_spec=pltpu.PrefetchScalarGridSpec(
            num_scalar_prefetch=1,
            grid=(layers, parts),
            in_specs=[spec(i, step) for i in range(count) for step in (0, 1)],
            out_specs=[out] * count,
        ),
        cost_estimate=pl.CostEstimate(
            flops=count * size // 4, bytes_accessed=3 * count * size, transcendentals=0
        ),
        name="extract",
    )(cols, *([specimen] * (2 * count)))


def pick(depth, at_zero, at_one, dst, sem):
    @pl.when(depth == 0)
    def _():
        pltpu.make_async_copy(at_zero, dst, sem).start()

    @pl.when(depth != 0)
    def _():
        pltpu.make_async_copy(at_one, dst, sem).start()

    return pltpu.make_async_copy(at_zero, dst, sem)


def fetch(scal, sources, patches, third, own, sems):
    rows = third.shape[2]
    depth = scal[0]
    lower = patches.at[:, :, pl.ds(rows, rows), :]
    copies = [
        pick(depth, sources[0], sources[1], lower, sems.at[0]),
        pick(depth, sources[2], sources[3], third, sems.at[1]),
        pick(depth, sources[4], sources[5], own, sems.at[2]),
    ]
    return copies


def merge(scal, patches, third, own):
    layers, parts, rows, patch = third.shape
    row = lax.broadcasted_iota(jnp.int32, (rows, patch), 0)
    from_own = (row < scal[2]) == (scal[1] == 1)
    for s in range(layers):
        for c in range(parts):
            patches[s, c, :rows] = jnp.where(from_own, own[s, c], third[s, c])


def first_kernel(scal, probe, kernel, table, *refs):
    sources, refs = refs[:6], refs[6:]
    patches, waves, rolled, third, own, cur, sems = refs
    copies = fetch(scal, sources, patches, third, own, sems)
    patch = probe.shape[-1]
    for c in range(2):
        turned = pltpu.roll(probe[c], scal[2], 0)
        turned = pltpu.roll(turned, scal[3] % patch, 1)
        rolled[c] = turned
        cur[c] = turned
    for copy in copies:
        copy.wait()
    merge(scal, patches, third, own)

    def step(s, unused):
        a, b = times(patches.at[s], cur[0], cur[1], False)
        a, b = forward(a, b, table)
        a, b = times(kernel, a, b, False)
        a, b = inverse(a, b, table)
        cur[0], cur[1] = a, b
        waves[s, 0], waves[s, 1] = a, b
        return unused

    lax.fori_loop(0, patches.shape[0], step, 0)


def put_grad(grad_top, grad_low, s, a, b):
    rows = grad_top.shape[2]
    grad_top[s, 0], grad_top[s, 1] = a[:rows], b[:rows]
    grad_low[s, 0], grad_low[s, 1] = a[rows:], b[rows:]


def second_kernel(scal, kernel, table, target, waves, *refs):
    sources, refs = refs[:6], refs[6:]
    grad_top, grad_low, leaving, patches, third, own, cur, last, sems = refs
    copies = fetch(scal, sources, patches, third, own, sems)
    for copy in copies:
        copy.wait()
    merge(scal, patches, third, own)
    entry = waves.at[1]
    a, b = times(patches.at[0], entry[0], entry[1], False)
    cur[0], cur[1] = a, b

    def step(s, unused):
        a, b = forward(cur[0], cur[1], table)
        middle = s == 1
        residue = 2.0 * (a * a + b * b - target[...])
        kr = jnp.where(middle, residue, kernel[0])
        ki = jnp.where(middle, 0.0, jnp.where(s == 0, kernel[1], -kernel[1]))
        a, b = kr * a - ki * b, kr * b + ki * a
        a, b = inverse(a, b, table)
        cur[0], cur[1] = a, b

        @pl.when(s == 0)
        def _():
            a, b = cur[0], cur[1]
            last[0], last[1] = a, b
            cur[0], cur[1] = times(patches.at[1], a, b, False)

        @pl.when(s == 1)
        def _():
            a, b = cur[0], cur[1]
            put_grad(grad_top, grad_low, 1, *times(last, a, b, True))
            cur[0], cur[1] = times(patches.at[1], a, b, True)

        @pl.when(s == 2)
        def _():
            a, b = cur[0], cur[1]
            put_grad(grad_top, grad_low, 0, *times(entry, a, b, True))
            leaving[0], leaving[1] = times(patches.at[0], a, b, True)

        return unused

    lax.fori_loop(0, 3, step, 0)


def third_kernel(kernel, table, waves, rolled, patches, entering, grad_top, grad_low, cur):
    cur[...] = entering[...]

    def step(s, unused):
        a, b = forward(cur[0], cur[1], table)
        a, b = times(kernel, a, b, True)
        a, b = inverse(a, b, table)
        cur[0], cur[1] = a, b

        @pl.when(s == 0)
        def _():
            a, b = cur[0], cur[1]
            put_grad(grad_top, grad_low, 1, *times(waves.at[0], a, b, True))
            cur[0], cur[1] = times(patches.at[1], a, b, True)

        @pl.when(s == 1)
        def _():
            put_grad(grad_top, grad_low, 0, *times(rolled, cur[0], cur[1], True))

        return unused

    lax.fori_loop(0, 2, step, 0)


def gather_kernel(scal, *refs):
    sources, (out, windows, total, sems, out_sems) = refs[:12], refs[12:]
    count = 6
    layers, parts, rows, patch = windows.shape[1:]
    final = total.shape[3] // patch - 1
    copies = [
        pick(scal[0], sources[2 * i], sources[2 * i + 1], windows.at[i], sems.at[i])
        for i in range(count)
    ]
    row = lax.broadcasted_iota(jnp.int32, (rows, patch), 0)
    lane = lax.broadcasted_iota(jnp.int32, (rows, patch), 1)
    odd = scal[1] == 1
    total[...] = jnp.zeros_like(total)
    for copy in copies:
        copy.wait()
    sends = []
    for s in range(layers):
        for c in range(parts):
            for i in range(count):
                column = scal[2 + 2 * i]
                value = windows[i, s, c]
                if i >= 2:
                    above = row < scal[3 + 2 * i]
                    keep = (above == odd) if i < 4 else (above != odd)
                    value = jnp.where(keep, value, 0.0)
                block, shift = column // patch, column % patch
                near = pl.ds(pl.multiple_of(block * patch, patch), patch)
                far = pl.ds(pl.multiple_of(jnp.minimum(block + 1, final) * patch, patch), patch)
                total[s, c, :, near] += jnp.where(lane < shift, 0.0, value)
                total[s, c, :, far] += jnp.where(lane < shift, value, 0.0)
            copy = pltpu.make_async_copy(total.at[s, c], out.at[s, c], out_sems.at[s, c])
            copy.start()
            sends.append(copy)
    for copy in sends:
        copy.wait()


def local(specimen, scan_offsets, probe_wave, fresnel_phase, measured):
    layers, parts, rows, width = specimen.shape
    patch = probe_wave.shape[-1]
    tiles, depths = lax.axis_size("tile"), lax.axis_size("depth")
    assert depths == 2 and layers == 2 and scan_offsets.shape[0] == depths
    assert tiles % 2 == 0 and patch == 2 * rows and width % patch == 0
    tile, depth = lax.axis_index("tile"), lax.axis_index("depth")
    parity = tile % 2

    swap = [(t, t ^ 1) for t in range(tiles)]
    other = [(t, t + 1) for t in range(1, tiles - 1, 2)] + [(t, t - 1) for t in range(2, tiles, 2)]
    outward = [(t, t + 2) for t in range(1, tiles - 2, 2)] + [
        (t, t - 2) for t in range(2, tiles, 2)
    ]
    homeward = [(b, a) for a, b in outward]
    stay = [(t, t) for t in range(tiles)]

    def send(value, pairs, *hops):
        return lax.ppermute(
            value, AXES, [(a * tiles + s, b * tiles + t) for a, b in hops for s, t in pairs]
        )

    their = lax.ppermute(scan_offsets, "tile", other)
    partner = lax.ppermute(scan_offsets, "tile", swap)
    target = lax.ppermute(
        lax.dynamic_index_in_dim(measured, depth, 0, keepdims=False), "tile", swap
    )
    order = jnp.stack([depth, 1 - depth])
    own_cols = scan_offsets[order, 1]
    their_cols, their_rows = their[order, 1], their[order, 0]
    part_cols, part_rows = partner[order, 1], partner[order, 0]
    part_rows = part_rows - ((tile ^ 1) - 1) * rows
    their_tile = jnp.where(parity == 1, tile + 1, tile - 1)
    their_rows = their_rows - (their_tile - 1) * rows

    table = jnp.asarray(dft_tables(patch))
    places = np.concatenate([np.arange(0, patch, 2), np.arange(1, patch, 2)])
    pick_one = jnp.asarray(np.eye(patch, dtype=np.float32)[places])

    def reorder(x):
        x = jnp.dot(pick_one, x, precision=lax.Precision.HIGHEST)
        return jnp.dot(x, pick_one.T, precision=lax.Precision.HIGHEST)

    phase = reorder(fresnel_phase)
    kernel = jnp.stack([jnp.cos(phase), jnp.sin(phase)], 0)
    target = reorder(target)

    mid_keep, mid_swap = extract(specimen, own_cols, patch)
    mids = [
        send(mid_keep, swap, (0, 0)),
        send(mid_swap, swap, (0, 1)),
    ]
    far_keep, far_swap, near_keep, near_swap = extract(
        specimen, cat([their_cols, part_cols]), patch
    )
    fars = [
        send(far_keep, outward, (0, 0)),
        send(far_swap, outward, (0, 1)),
    ]
    near_other = send(near_swap, stay, (0, 1), (1, 0))
    mids += [send(mid_swap, swap, (1, 0)), send(mid_keep, swap, (1, 1))]
    fars += [send(far_swap, outward, (1, 0)), send(far_keep, outward, (1, 1))]

    scal = jnp.stack([depth, parity, part_rows[0], part_cols[0]]).astype(jnp.int32)
    pair = jax.ShapeDtypeStruct((2, patch, patch), F32)
    slab = jax.ShapeDtypeStruct((layers, 2, patch, patch), F32)
    band = jax.ShapeDtypeStruct((layers, 2, rows, patch), F32)
    full_v = pltpu.VMEM((layers, 2, patch, patch), F32)
    band_v = pltpu.VMEM((layers, 2, rows, patch), F32)
    pair_v = pltpu.VMEM((2, patch, patch), F32)
    work = 12 * 2 * patch**3
    patches, waves, rolled = pl.pallas_call(
        first_kernel,
        out_shape=[slab, slab, pair],
        in_specs=[SMEM, VMEM, VMEM, VMEM] + [ANY] * 6,
        out_specs=[VMEM] * 3,
        scratch_shapes=[band_v, band_v, pair_v, pltpu.SemaphoreType.DMA((3,))],
        cost_estimate=pl.CostEstimate(flops=4 * work, bytes_accessed=6 << 20, transcendentals=0),
        name="first",
    )(scal, probe_wave, kernel, table, mids[0], mids[1], fars[0], fars[1], near_keep, near_other)
    top_b, low_b, leaving = pl.pallas_call(
        second_kernel,
        out_shape=[band, band, pair],
        in_specs=[SMEM, VMEM, VMEM, VMEM, VMEM] + [ANY] * 6,
        out_specs=[VMEM] * 3,
        scratch_shapes=[full_v, band_v, band_v, pair_v, pair_v, pltpu.SemaphoreType.DMA((3,))],
        cost_estimate=pl.CostEstimate(flops=6 * work, bytes_accessed=6 << 20, transcendentals=0),
        name="second",
    )(scal, kernel, table, target, waves, mids[2], mids[3], fars[2], fars[3], near_other, near_keep)
    low_back = [None, send(low_b, swap, (1, 1)), None, send(low_b, swap, (0, 1))]
    top_back = [None, send(top_b, homeward, (1, 1)), None, send(top_b, homeward, (0, 1))]
    top_b_other = send(top_b, stay, (0, 1))
    top_c, low_c = pl.pallas_call(
        third_kernel,
        out_shape=[band, band],
        in_specs=[VMEM] * 6,
        out_specs=[VMEM] * 2,
        scratch_shapes=[pair_v],
        cost_estimate=pl.CostEstimate(flops=4 * work, bytes_accessed=6 << 20, transcendentals=0),
        name="third",
    )(kernel, table, waves, rolled, patches, leaving)
    low_back[0], low_back[2] = send(low_c, swap, (0, 0)), send(low_c, swap, (1, 0))
    top_back[0], top_back[2] = send(top_c, homeward, (0, 0)), send(top_c, homeward, (1, 0))
    top_c_other = send(top_c, stay, (1, 0))

    zero = jnp.zeros((), jnp.int32)
    places = jnp.stack(
        [depth, parity]
        + [own_cols[0], zero, own_cols[1], zero]
        + [part_cols[0], part_rows[0], part_cols[1], part_rows[1]]
        + [their_cols[0], their_rows[0], their_cols[1], their_rows[1]]
    ).astype(jnp.int32)
    return pl.pallas_call(
        gather_kernel,
        out_shape=jax.ShapeDtypeStruct(specimen.shape, F32),
        in_specs=[SMEM] + [ANY] * 12,
        out_specs=ANY,
        scratch_shapes=[
            pltpu.VMEM((6, layers, 2, rows, patch), F32),
            pltpu.VMEM(specimen.shape, F32),
            pltpu.SemaphoreType.DMA((6,)),
            pltpu.SemaphoreType.DMA((layers, 2)),
        ],
        cost_estimate=pl.CostEstimate(flops=6 << 20, bytes_accessed=7 << 20, transcendentals=0),
        name="gather",
    )(places, *low_back, top_c, top_b, top_c_other, top_b_other, *top_back)


def solution(mesh):
    placed = (P("depth", None, "tile", None), P("tile", None), P(), P(), P("tile", None, None))
    return jax.shard_map(
        local, mesh=mesh, in_specs=placed, out_specs=P("depth", None, "tile", None), check_vma=False
    )
```

```python
import functools

import jax
import jax.numpy as jnp
import numpy as np
from jax import lax
from jax.experimental import pallas as pl
from jax.experimental.pallas import tpu as pltpu
from jax.sharding import PartitionSpec as P


F32 = jnp.float32
BF16 = jnp.bfloat16
AXES = ("depth", "tile")
ANY = pl.BlockSpec(memory_space=pl.ANY)
VMEM = pl.BlockSpec(memory_space=pltpu.VMEM)
HBM = pl.BlockSpec(memory_space=pltpu.HBM)
SMEM = pl.BlockSpec(memory_space=pltpu.SMEM)
cat = jnp.concatenate


def limit(mebibytes):
    return pltpu.CompilerParams(vmem_limit_bytes=mebibytes << 20)


def dft_tables(extent):
    half = extent // 2
    row, col = np.arange(half)[:, None], np.arange(half)[None, :]
    blocks = []
    for parity in (0, 1):
        turn = (row * (2 * col + parity)) % extent
        wave = np.exp(-2j * np.pi * turn / extent) / np.sqrt(extent)
        blocks.append(np.block([[wave.real, wave.imag], [-wave.imag, wave.real]]))
    table = np.stack([blocks[0], blocks[1], blocks[0].T, blocks[1].T])
    high = table.astype(np.float32).astype(BF16)
    low = (table - high.astype(np.float64)).astype(np.float32).astype(BF16)
    return np.stack([high, low], 1)


def split(x):
    high = x.astype(BF16)
    return high, (x - high.astype(F32)).astype(BF16)


def dot(a, b):
    return jnp.dot(a, b, preferred_element_type=F32)


def rmul(x, table, which):
    high, low = split(x)
    t_high, t_low = table[which, 0], table[which, 1]
    return dot(high, t_high) + (dot(low, t_high) + dot(high, t_low))


def lmul(table, which, x):
    high, low = split(x)
    t_high, t_low = table[which, 0], table[which, 1]
    return dot(t_high, high) + (dot(t_high, low) + dot(t_low, high))


def forward(xr, xi, table):
    h = xr.shape[0] // 2
    e = rmul(cat([xr[:, :h] + xr[:, h:], xi[:, :h] + xi[:, h:]], 1), table, 0)
    o = rmul(cat([xr[:, :h] - xr[:, h:], xi[:, :h] - xi[:, h:]], 1), table, 1)
    yr, yi = cat([e[:, :h], o[:, :h]], 1), cat([e[:, h:], o[:, h:]], 1)
    e = lmul(table, 2, cat([yr[:h] + yr[h:], yi[:h] + yi[h:]], 0))
    o = lmul(table, 3, cat([yr[:h] - yr[h:], yi[:h] - yi[h:]], 0))
    return cat([e[:h], o[:h]], 0), cat([e[h:], o[h:]], 0)


def inverse(xr, xi, table):
    h = xr.shape[0] // 2
    e = lmul(table, 0, cat([xr[:h], xi[:h]], 0))
    o = lmul(table, 1, cat([xr[h:], xi[h:]], 0))
    yr = cat([e[:h] + o[:h], e[:h] - o[:h]], 0)
    yi = cat([e[h:] + o[h:], e[h:] - o[h:]], 0)
    e = rmul(cat([yr[:, :h], yi[:, :h]], 1), table, 2)
    o = rmul(cat([yr[:, h:], yi[:, h:]], 1), table, 3)
    return (
        cat([e[:, :h] + o[:, :h], e[:, :h] - o[:, :h]], 1),
        cat([e[:, h:] + o[:, h:], e[:, h:] - o[:, h:]], 1),
    )


def times(ref, a, b, conj):
    pr, pi = ref[0], ref[1]
    if conj:
        return pr * a + pi * b, pr * b - pi * a
    return pr * a - pi * b, pr * b + pi * a


def place(column, patch, width):
    block = jnp.minimum(column // patch, width // patch - 2)
    return pl.multiple_of(block * patch, patch), column - block * patch


def extract_kernel(count, *refs):
    offsets, specimen = refs[:count], refs[count]
    outs, (wide, sems) = refs[count + 1 : 3 * count + 1], refs[3 * count + 1 :]
    depth = lax.axis_index("depth")
    layers, parts, rows = specimen.shape[:3]
    patch = outs[0].shape[3]
    shifts, copies = [], []
    for i in range(2 * count):
        position = depth if i % 2 == 0 else 1 - depth
        start, shift = place(offsets[i // 2][position, 1], patch, specimen.shape[3])
        shifts.append(shift)
        for s in range(layers):
            copy = pltpu.make_async_copy(
                specimen.at[s, :, :, pl.ds(start, 2 * patch)], wide.at[i, s], sems.at[i, s]
            )
            copy.start()
            copies.append(copy)
    lane = lax.broadcasted_iota(jnp.int32, (rows, patch), 1)
    for i in range(2 * count):
        for s in range(layers):
            copies[i * layers + s].wait()
            for c in range(parts):
                outs[i][s, c] = jnp.where(
                    lane < shifts[i], wide[i, s, c, :, patch:], wide[i, s, c, :, :patch]
                )


def extract(specimen, offsets, patch):
    count = len(offsets)
    layers, parts, rows, _ = specimen.shape
    size = 2 * count * layers * parts * rows * patch
    return pl.pallas_call(
        functools.partial(extract_kernel, count),
        out_shape=[jax.ShapeDtypeStruct((layers, parts, rows, patch), F32)] * (2 * count),
        in_specs=[SMEM] * count + [HBM],
        out_specs=[VMEM] * (2 * count),
        scratch_shapes=[
            pltpu.VMEM((2 * count, layers, parts, rows, 2 * patch), F32),
            pltpu.SemaphoreType.DMA((2 * count, layers)),
        ],
        cost_estimate=pl.CostEstimate(flops=size, bytes_accessed=12 * size, transcendentals=0),
        compiler_params=limit(16),
        name="extract",
    )(*offsets, pltpu.with_memory_space_constraint(specimen, pltpu.HBM))


def top_row(offsets, position, holder, rows):
    return offsets[position, 0] - (holder - 1) * rows


def work_kernel(core, offsets, probe, kernel, table, target, *refs):
    mids, fars, nears, refs = refs[0:2], refs[2:4], refs[4:6], refs[6:]
    tops, lows, (patches, waves, cur, third, own, sems) = refs[0:2], refs[2:4], refs[4:]
    count = patches.shape[0]
    layers, parts, rows, patch = third.shape[1:]
    groups = (core, 1 - core)

    @pl.when(lax.axis_index("depth") == core)
    def _():
        tile = lax.axis_index("tile")
        copies = []
        for i, group in enumerate(groups):
            part = patches.at[pl.ds(group * layers, layers), :, pl.ds(rows, rows), :]
            copies += [
                pltpu.make_async_copy(mids[i], part, sems.at[i, 0]),
                pltpu.make_async_copy(fars[i], third.at[group], sems.at[i, 1]),
                pltpu.make_async_copy(nears[i], own.at[group], sems.at[i, 2]),
            ]
        for copy in copies:
            copy.start()
        down = top_row(offsets, core, tile ^ 1, rows)
        right = offsets[core, 1] % patch
        for c in range(2):
            waves[0, c] = pltpu.roll(pltpu.roll(probe[c], down, 0), right, 1)
        row = lax.broadcasted_iota(jnp.int32, (rows, patch), 0)
        from_own = (row < down) == (tile % 2 == 1)
        for copy in copies:
            copy.wait()
        for s in range(count):
            for c in range(parts):
                g, r = divmod(s, layers)
                patches[s, c, :rows] = jnp.where(from_own, own[g, r, c], third[g, r, c])
        cur[0], cur[1] = times(patches.at[0], waves[0, 0], waves[0, 1], False)

        def step(s, unused):
            a, b = forward(cur[0], cur[1], table)
            exit_step = s == count - 1
            residue = 2.0 * (a * a + b * b - target[...])
            kr = jnp.where(exit_step, residue, kernel[0])
            ki = jnp.where(exit_step, 0.0, jnp.where(s < count, kernel[1], -kernel[1]))
            a, b = kr * a - ki * b, kr * b + ki * a
            cur[0], cur[1] = inverse(a, b, table)

            @pl.when(s < count - 1)
            def _():
                waves[s + 1] = cur[...]
                cur[0], cur[1] = times(patches.at[s + 1], cur[0], cur[1], False)

            @pl.when(s >= count - 1)
            def _():
                k = 2 * (count - 1) - s
                a, b = times(waves.at[k], cur[0], cur[1], True)
                for i, group in enumerate(groups):

                    @pl.when(k // layers == group)
                    def _():
                        r = k % layers
                        tops[i][r, 0], tops[i][r, 1] = a[:rows], b[:rows]
                        lows[i][r, 0], lows[i][r, 1] = a[rows:], b[rows:]

                cur[0], cur[1] = times(patches.at[k], cur[0], cur[1], True)

            return unused

        lax.fori_loop(0, 2 * count - 1, step, 0)


def work(core, offsets, probe, kernel, table, target, *sources):
    layers, parts, rows, patch = sources[0].shape
    band = jax.ShapeDtypeStruct(sources[0].shape, F32)
    full_v = pltpu.VMEM((2 * layers, parts, patch, patch), F32)
    band_v = pltpu.VMEM((2, layers, parts, rows, patch), F32)
    flops = 28 * layers * 12 * patch**3
    return pl.pallas_call(
        functools.partial(work_kernel, core),
        out_shape=[band] * 4,
        in_specs=[SMEM] + [VMEM] * 4 + [ANY] * 6,
        out_specs=[VMEM] * 4,
        scratch_shapes=[
            full_v,
            full_v,
            pltpu.VMEM((parts, patch, patch), F32),
            band_v,
            band_v,
            pltpu.SemaphoreType.DMA((2, 3)),
        ],
        cost_estimate=pl.CostEstimate(flops=flops, bytes_accessed=8 << 20, transcendentals=0),
        compiler_params=limit(28),
        name="work",
    )(offsets, probe, kernel, table, target, *sources)


def pick(depth, at_zero, at_one, dst, sem):
    @pl.when(depth == 0)
    def _():
        pltpu.make_async_copy(at_zero, dst, sem).start()

    @pl.when(depth != 0)
    def _():
        pltpu.make_async_copy(at_one, dst, sem).start()

    return pltpu.make_async_copy(at_zero, dst, sem)


def gather_kernel(own, partner, their, *refs):
    sources, (out, windows, total, sems, out_sems) = refs[:12], refs[12:]
    layers, parts, rows, patch = windows.shape[1:]
    depth, tile = lax.axis_index("depth"), lax.axis_index("tile")
    copies = [
        pick(depth, sources[2 * i], sources[2 * i + 1], windows.at[i], sems.at[i])
        for i in range(6)
    ]
    row = lax.broadcasted_iota(jnp.int32, (rows, patch), 0)
    lane = lax.broadcasted_iota(jnp.int32, (rows, patch), 1)
    odd = tile % 2 == 1
    total[...] = jnp.zeros_like(total)
    facts = []
    for i in range(6):
        offsets = (own, partner, their)[i // 2]
        position = depth if i % 2 == 0 else 1 - depth
        holder = (tile, tile ^ 1, jnp.where(odd, tile + 1, tile - 1))[i // 2]
        start, shift = place(offsets[position, 1], patch, total.shape[3])
        facts.append((start, shift, top_row(offsets, position, holder, rows)))
    for copy in copies:
        copy.wait()
    sends = []
    for s in range(layers):
        for c in range(parts):
            for i in range(6):
                start, shift, down = facts[i]
                value = windows[i, s, c]
                if i >= 2:
                    above = row < down
                    keep = (above == odd) if i < 4 else (above != odd)
                    value = jnp.where(keep, value, 0.0)
                near = pl.ds(start, patch)
                far = pl.ds(pl.multiple_of(start + patch, patch), patch)
                total[s, c, :, near] += jnp.where(lane < shift, 0.0, value)
                total[s, c, :, far] += jnp.where(lane < shift, value, 0.0)
            copy = pltpu.make_async_copy(total.at[s, c], out.at[s, c], out_sems.at[s, c])
            copy.start()
            sends.append(copy)
    for copy in sends:
        copy.wait()


def local(specimen, scan_offsets, probe_wave, fresnel_phase, measured):
    layers, parts, rows, width = specimen.shape
    patch = probe_wave.shape[-1]
    tiles, depths = lax.axis_size("tile"), lax.axis_size("depth")
    assert depths == 2 and scan_offsets.shape[0] == depths
    assert tiles % 2 == 0 and patch == 2 * rows and width % patch == 0
    depth = lax.axis_index("depth")

    swap = [(t, t ^ 1) for t in range(tiles)]
    other = [(t, t + 1) for t in range(1, tiles - 1, 2)] + [(t, t - 1) for t in range(2, tiles, 2)]
    outward = [(t, t + 2) for t in range(1, tiles - 2, 2)] + [
        (t, t - 2) for t in range(2, tiles, 2)
    ]
    homeward = [(b, a) for a, b in outward]
    stay = [(t, t) for t in range(tiles)]
    same, cross = [(0, 0), (1, 1)], [(0, 1), (1, 0)]

    def send(value, pairs, hops):
        return lax.ppermute(
            value, AXES, [(a * tiles + s, b * tiles + t) for a, b in hops for s, t in pairs]
        )

    their = send(scan_offsets, other, same)
    target = lax.dynamic_index_in_dim(measured, depth, 0, keepdims=False)
    target = send(target, swap, same)
    partner = send(scan_offsets, swap, same)

    table = jnp.asarray(dft_tables(patch))
    places = np.concatenate([np.arange(0, patch, 2), np.arange(1, patch, 2)])
    pick_one = jnp.asarray(np.eye(patch, dtype=np.float32)[places])

    def reorder(x):
        x = jnp.dot(pick_one, x, precision=lax.Precision.HIGHEST)
        return jnp.dot(x, pick_one.T, precision=lax.Precision.HIGHEST)

    phase = reorder(fresnel_phase)
    kernel = jnp.stack([jnp.cos(phase), jnp.sin(phase)], 0)
    their, kernel = lax.optimization_barrier((their, kernel))
    found = extract(specimen, [their, scan_offsets, partner], patch)
    far, mid, near = found[0:2], found[2:4], found[4:6]
    mids, fars = [], []
    for core in range(2):
        for step in range(2):
            hop = [((core + step) % 2, core)]
            mids.append(send(mid[step], swap, hop))
            fars.append(send(far[step], outward, hop))
    near_other = send(near[1], stay, cross)
    target = reorder(target)

    kept, others, lows, tops = [], [], [], []
    for core in range(2):
        grads = work(
            core, partner, probe_wave, kernel, table, target,
            *mids[2 * core : 2 * core + 2], *fars[2 * core : 2 * core + 2],
            near[0], near_other,
        )
        for step in range(2):
            hop = [(core, (core + step) % 2)]
            tops.append(send(grads[step], homeward, hop))
            lows.append(send(grads[2 + step], swap, hop))
        kept.append(grads[0])
        others.append(send(grads[1], stay, [(core, 1 - core)]))
    windows = [lows[0], lows[2], lows[3], lows[1]]
    windows += [kept[0], kept[1], others[1], others[0]]
    windows += [tops[0], tops[2], tops[3], tops[1]]
    return pl.pallas_call(
        gather_kernel,
        out_shape=jax.ShapeDtypeStruct(specimen.shape, F32),
        in_specs=[SMEM] * 3 + [ANY] * 12,
        out_specs=ANY,
        scratch_shapes=[
            pltpu.VMEM((6, layers, parts, rows, patch), F32),
            pltpu.VMEM(specimen.shape, F32),
            pltpu.SemaphoreType.DMA((6,)),
            pltpu.SemaphoreType.DMA((layers, parts)),
        ],
        cost_estimate=pl.CostEstimate(flops=6 << 20, bytes_accessed=7 << 20, transcendentals=0),
        compiler_params=limit(16),
        name="gather",
    )(scan_offsets, partner, their, *windows)


def solution(mesh):
    placed = (P("depth", None, "tile", None), P("tile", None), P(), P(), P("tile", None, None))

    return jax.shard_map(
        local,
        mesh=mesh,
        in_specs=placed,
        out_specs=P("depth", None, "tile", None),
        check_vma=False,
    )
```

```python
import functools

import jax
import jax.numpy as jnp
import numpy as np
from jax import lax
from jax.experimental import pallas as pl
from jax.experimental.pallas import tpu as pltpu
from jax.sharding import PartitionSpec as P


F32 = jnp.float32
BF16 = jnp.bfloat16
AXES = ("depth", "tile")
ANY = pl.BlockSpec(memory_space=pl.ANY)
VMEM = pl.BlockSpec(memory_space=pltpu.VMEM)
HBM = pl.BlockSpec(memory_space=pltpu.HBM)
SMEM = pl.BlockSpec(memory_space=pltpu.SMEM)
cat = jnp.concatenate


def limit(mebibytes):
    return pltpu.CompilerParams(vmem_limit_bytes=mebibytes << 20)


def dft_tables(extent):
    half = extent // 2
    row, col = np.arange(half)[:, None], np.arange(half)[None, :]
    blocks = []
    for parity in (0, 1):
        turn = (row * (2 * col + parity)) % extent
        wave = np.exp(-2j * np.pi * turn / extent) / np.sqrt(extent)
        blocks.append(np.block([[wave.real, wave.imag], [-wave.imag, wave.real]]))
    table = np.stack([blocks[0], blocks[1], blocks[0].T, blocks[1].T])
    high = table.astype(np.float32).astype(BF16)
    low = (table - high.astype(np.float64)).astype(np.float32).astype(BF16)
    return np.stack([high, low], 1)


def split(x):
    high = x.astype(BF16)
    return high, (x - high.astype(F32)).astype(BF16)


def dot(a, b):
    return jnp.dot(a, b, preferred_element_type=F32)


def rmul(x, table, which):
    high, low = split(x)
    t_high, t_low = table[which, 0], table[which, 1]
    return dot(high, t_high) + (dot(low, t_high) + dot(high, t_low))


def lmul(table, which, x):
    high, low = split(x)
    t_high, t_low = table[which, 0], table[which, 1]
    return dot(t_high, high) + (dot(t_high, low) + dot(t_low, high))


def forward(xr, xi, table):
    h = xr.shape[0] // 2
    e = rmul(cat([xr[:, :h] + xr[:, h:], xi[:, :h] + xi[:, h:]], 1), table, 0)
    o = rmul(cat([xr[:, :h] - xr[:, h:], xi[:, :h] - xi[:, h:]], 1), table, 1)
    yr, yi = cat([e[:, :h], o[:, :h]], 1), cat([e[:, h:], o[:, h:]], 1)
    e = lmul(table, 2, cat([yr[:h] + yr[h:], yi[:h] + yi[h:]], 0))
    o = lmul(table, 3, cat([yr[:h] - yr[h:], yi[:h] - yi[h:]], 0))
    return cat([e[:h], o[:h]], 0), cat([e[h:], o[h:]], 0)


def inverse(xr, xi, table):
    h = xr.shape[0] // 2
    e = lmul(table, 0, cat([xr[:h], xi[:h]], 0))
    o = lmul(table, 1, cat([xr[h:], xi[h:]], 0))
    yr = cat([e[:h] + o[:h], e[:h] - o[:h]], 0)
    yi = cat([e[h:] + o[h:], e[h:] - o[h:]], 0)
    e = rmul(cat([yr[:, :h], yi[:, :h]], 1), table, 2)
    o = rmul(cat([yr[:, h:], yi[:, h:]], 1), table, 3)
    return (
        cat([e[:, :h] + o[:, :h], e[:, :h] - o[:, :h]], 1),
        cat([e[:, h:] + o[:, h:], e[:, h:] - o[:, h:]], 1),
    )


def times(ref, a, b, conj):
    pr, pi = ref[0], ref[1]
    if conj:
        return pr * a + pi * b, pr * b - pi * a
    return pr * a - pi * b, pr * b + pi * a


def place(column, patch, width):
    block = jnp.minimum(column // patch, width // patch - 2)
    return pl.multiple_of(block * patch, patch), column - block * patch


def extract_kernel(count, *refs):
    offsets, specimen = refs[:count], refs[count]
    outs, (wide, sems) = refs[count + 1 : 3 * count + 1], refs[3 * count + 1 :]
    depth = lax.axis_index("depth")
    layers, parts, rows = specimen.shape[:3]
    patch = outs[0].shape[3]
    shifts, copies = [], []
    for i in range(2 * count):
        position = depth if i % 2 == 0 else 1 - depth
        start, shift = place(offsets[i // 2][position, 1], patch, specimen.shape[3])
        shifts.append(shift)
        for s in range(layers):
            copy = pltpu.make_async_copy(
                specimen.at[s, :, :, pl.ds(start, 2 * patch)], wide.at[i, s], sems.at[i, s]
            )
            copy.start()
            copies.append(copy)
    lane = lax.broadcasted_iota(jnp.int32, (rows, patch), 1)
    for i in range(2 * count):
        for s in range(layers):
            copies[i * layers + s].wait()
            for c in range(parts):
                outs[i][s, c] = jnp.where(
                    lane < shifts[i], wide[i, s, c, :, patch:], wide[i, s, c, :, :patch]
                )


def extract(specimen, offsets, patch):
    count = len(offsets)
    layers, parts, rows, _ = specimen.shape
    size = 2 * count * layers * parts * rows * patch
    return pl.pallas_call(
        functools.partial(extract_kernel, count),
        out_shape=[jax.ShapeDtypeStruct((layers, parts, rows, patch), F32)] * (2 * count),
        in_specs=[SMEM] * count + [HBM],
        out_specs=[VMEM] * (2 * count),
        scratch_shapes=[
            pltpu.VMEM((2 * count, layers, parts, rows, 2 * patch), F32),
            pltpu.SemaphoreType.DMA((2 * count, layers)),
        ],
        cost_estimate=pl.CostEstimate(flops=size, bytes_accessed=12 * size, transcendentals=0),
        compiler_params=limit(16),
        name="extract",
    )(*offsets, pltpu.with_memory_space_constraint(specimen, pltpu.HBM))


def top_row(offsets, position, holder, rows):
    return offsets[position, 0] - (holder - 1) * rows


def work_kernel(core, offsets, probe, kernel, table, target, *refs):
    mids, fars, nears, refs = refs[0:2], refs[2:4], refs[4:6], refs[6:]
    tops, lows, (patches, waves, cur) = refs[0:2], refs[2:4], refs[4:]
    count = patches.shape[0]
    layers, parts, rows, patch = mids[0].shape
    groups = (core, 1 - core)

    @pl.when(lax.axis_index("depth") == core)
    def _():
        tile = lax.axis_index("tile")
        down = top_row(offsets, core, tile ^ 1, rows)
        right = offsets[core, 1] % patch
        for c in range(2):
            waves[0, c] = pltpu.roll(pltpu.roll(probe[c], down, 0), right, 1)
        row = lax.broadcasted_iota(jnp.int32, (rows, patch), 0)
        from_own = (row < down) == (tile % 2 == 1)
        for i, group in enumerate(groups):
            for r in range(layers):
                for c in range(parts):
                    s = group * layers + r
                    patches[s, c, :rows] = jnp.where(from_own, nears[i][r, c], fars[i][r, c])
                    patches[s, c, rows:] = mids[i][r, c]
        cur[0], cur[1] = times(patches.at[0], waves[0, 0], waves[0, 1], False)

        def step(s, unused):
            a, b = forward(cur[0], cur[1], table)
            exit_step = s == count - 1
            residue = 2.0 * (a * a + b * b - target[...])
            kr = jnp.where(exit_step, residue, kernel[0])
            ki = kernel[1] * jnp.where(exit_step, 0.0, jnp.where(s < count, 1.0, -1.0))
            a, b = kr * a - ki * b, kr * b + ki * a
            cur[0], cur[1] = inverse(a, b, table)

            @pl.when(s < count - 1)
            def _():
                waves[s + 1] = cur[...]
                cur[0], cur[1] = times(patches.at[s + 1], cur[0], cur[1], False)

            @pl.when(s >= count - 1)
            def _():
                k = 2 * (count - 1) - s
                a, b = times(waves.at[k], cur[0], cur[1], True)
                for i, group in enumerate(groups):

                    @pl.when(k // layers == group)
                    def _():
                        r = k % layers
                        tops[i][r, 0], tops[i][r, 1] = a[:rows], b[:rows]
                        lows[i][r, 0], lows[i][r, 1] = a[rows:], b[rows:]

                cur[0], cur[1] = times(patches.at[k], cur[0], cur[1], True)

            return unused

        lax.fori_loop(0, 2 * count - 1, step, 0)


def work(core, offsets, probe, kernel, table, target, *sources):
    layers, parts, _, patch = sources[0].shape
    band = jax.ShapeDtypeStruct(sources[0].shape, F32)
    full_v = pltpu.VMEM((2 * layers, parts, patch, patch), F32)
    flops = 28 * layers * 12 * patch**3
    return pl.pallas_call(
        functools.partial(work_kernel, core),
        out_shape=[band] * 4,
        in_specs=[SMEM] + [VMEM] * 10,
        out_specs=[VMEM] * 4,
        scratch_shapes=[full_v, full_v, pltpu.VMEM((parts, patch, patch), F32)],
        cost_estimate=pl.CostEstimate(flops=flops, bytes_accessed=8 << 20, transcendentals=0),
        compiler_params=limit(28),
        name="work",
    )(offsets, probe, kernel, table, target, *sources)


def gather_kernel(own, partner, their, *refs):
    sources, (out, total, out_sems) = refs[:12], refs[12:]
    layers, parts, rows, patch = sources[0].shape
    depth, tile = lax.axis_index("depth"), lax.axis_index("tile")
    row = lax.broadcasted_iota(jnp.int32, (rows, patch), 0)
    lane = lax.broadcasted_iota(jnp.int32, (rows, patch), 1)
    odd = tile % 2 == 1
    total[...] = jnp.zeros_like(total)
    facts = []
    for i in range(6):
        offsets = (own, partner, their)[i // 2]
        position = depth if i % 2 == 0 else 1 - depth
        holder = (tile, tile ^ 1, jnp.where(odd, tile + 1, tile - 1))[i // 2]
        start, shift = place(offsets[position, 1], patch, total.shape[3])
        facts.append((start, shift, top_row(offsets, position, holder, rows)))
    sends = []
    for s in range(layers):
        for c in range(parts):
            for i in range(6):
                start, shift, down = facts[i]
                value = jnp.where(depth == 0, sources[2 * i][s, c], sources[2 * i + 1][s, c])
                if i >= 2:
                    above = row < down
                    keep = (above == odd) if i < 4 else (above != odd)
                    value = jnp.where(keep, value, 0.0)
                near = pl.ds(start, patch)
                far = pl.ds(pl.multiple_of(start + patch, patch), patch)
                total[s, c, :, near] += jnp.where(lane < shift, 0.0, value)
                total[s, c, :, far] += jnp.where(lane < shift, value, 0.0)
            copy = pltpu.make_async_copy(total.at[s, c], out.at[s, c], out_sems.at[s, c])
            copy.start()
            sends.append(copy)
    for copy in sends:
        copy.wait()


def local(specimen, scan_offsets, probe_wave, fresnel_phase, measured):
    layers, parts, rows, width = specimen.shape
    patch = probe_wave.shape[-1]
    tiles, depths = lax.axis_size("tile"), lax.axis_size("depth")
    assert depths == 2 and scan_offsets.shape[0] == depths
    assert tiles % 2 == 0 and patch == 2 * rows and width % patch == 0
    depth = lax.axis_index("depth")

    swap = [(t, t ^ 1) for t in range(tiles)]
    other = [(t, t + 1) for t in range(1, tiles - 1, 2)] + [(t, t - 1) for t in range(2, tiles, 2)]
    outward = [(t, t + 2) for t in range(1, tiles - 2, 2)] + [
        (t, t - 2) for t in range(2, tiles, 2)
    ]
    homeward = [(b, a) for a, b in outward]
    stay = [(t, t) for t in range(tiles)]
    same, cross = [(0, 0), (1, 1)], [(0, 1), (1, 0)]

    def send(value, pairs, hops):
        return lax.ppermute(
            value, AXES, [(a * tiles + s, b * tiles + t) for a, b in hops for s, t in pairs]
        )

    their = send(scan_offsets, other, same)
    target = lax.dynamic_index_in_dim(measured, depth, 0, keepdims=False)
    target = send(target, swap, same)
    partner = send(scan_offsets, swap, same)

    table = jnp.asarray(dft_tables(patch))
    places = np.concatenate([np.arange(0, patch, 2), np.arange(1, patch, 2)])
    pick_one = jnp.asarray(np.eye(patch, dtype=np.float32)[places])

    def reorder(x):
        x = jnp.dot(pick_one, x, precision=lax.Precision.HIGHEST)
        return jnp.dot(x, pick_one.T, precision=lax.Precision.HIGHEST)

    offsets = pltpu.with_memory_space_constraint(scan_offsets, pltpu.HBM)
    found = extract(specimen, [their, offsets], patch)
    far, mid = found[0:2], found[2:4]
    near = extract(specimen, [partner], patch)
    mids, fars = [], []
    for core in range(2):
        for step in range(2):
            hop = [((core + step) % 2, core)]
            mids.append(send(mid[step], swap, hop))
            fars.append(send(far[step], outward, hop))
    near_other = send(near[1], stay, cross)
    phase = reorder(fresnel_phase)
    kernel = jnp.stack([jnp.cos(phase), jnp.sin(phase)], 0)
    target = reorder(target)

    kept, others, lows, tops = [], [], [], []
    for core in range(2):
        grads = work(
            core, partner, probe_wave, kernel, table, target,
            *mids[2 * core : 2 * core + 2], *fars[2 * core : 2 * core + 2],
            near[0], near_other,
        )
        for step in range(2):
            hop = [(core, (core + step) % 2)]
            tops.append(send(grads[step], homeward, hop))
            lows.append(send(grads[2 + step], swap, hop))
        kept.append(grads[0])
        others.append(send(grads[1], stay, [(core, 1 - core)]))
    windows = [lows[0], lows[2], lows[3], lows[1]]
    windows += [kept[0], kept[1], others[1], others[0]]
    windows += [tops[0], tops[2], tops[3], tops[1]]
    return pl.pallas_call(
        gather_kernel,
        out_shape=jax.ShapeDtypeStruct(specimen.shape, F32),
        in_specs=[SMEM] * 3 + [VMEM] * 12,
        out_specs=ANY,
        scratch_shapes=[pltpu.VMEM(specimen.shape, F32), pltpu.SemaphoreType.DMA((layers, parts))],
        cost_estimate=pl.CostEstimate(flops=6 << 20, bytes_accessed=7 << 20, transcendentals=0),
        compiler_params=limit(16),
        name="gather",
    )(scan_offsets, partner, their, *windows)


def solution(mesh):
    placed = (P("depth", None, "tile", None), P("tile", None), P(), P(), P("tile", None, None))

    return jax.shard_map(
        local,
        mesh=mesh,
        in_specs=placed,
        out_specs=P("depth", None, "tile", None),
        check_vma=False,
    )
```
